256 devices in a mesh: pipe: 8 (over x, core), expert: 32 (over y, z).
Axes of the slice: x: 4, y: 4, z: 8, core: 2. Of those that a mesh axis runs over, the one named last changes fastest.
Arguments:
- acts: bfloat16 [8, 2, 2048, 2048], P('pipe', None, 'expert'), may hold values from -6 to 6
- out_grad: bfloat16 [2, 2048, 2048], P(None, 'expert'), may hold values from -6 to 6
- w_gate: bfloat16 [8, 32, 2048, 768], P('pipe', 'expert'), may hold values from -0.125 to 0.125
- w_up: bfloat16 [8, 32, 2048, 768], P('pipe', 'expert'), may hold values from -0.125 to 0.125
- w_down: bfloat16 [8, 32, 768, 2048], P('pipe', 'expert'), may hold values from -0.21875 to 0.21875
- routes: int32 [8, 2, 2048, 8], P('pipe', None, 'expert'), may hold values from 0 to 127, all different within a row
- gates: float32 [8, 2, 2048, 8], P('pipe', None, 'expert'), may hold values from 0.2 to 0.6
Outputs:
- in_grad: bfloat16 [8, 2, 2048, 2048], P('pipe', None, 'expert')
The draws below stay inside these ranges and needn't reach their ends.
Inputs may be any that keep to these rules, and one draw needn't show every extreme that they name: `routes`: each token's 8 choices name different experts, and every expert is chosen somewhere.
All inputs are finite; a program needn't handle non-finite values.
Results may differ from the reference program's by a relative error of at most 0.02.
Values may be sent and summed in bfloat16 or wider, within the bound.
A program may use at most 64 MiB of HBM per device.

```python
from functools import partial
import jax
import jax.numpy as jnp
from jax import lax

D = 2048
H = 768
EXPERTS = 128
TOP = 8
MICRO = 2
TOK_DEV = 64
CAP = 6
LIVE = 32
SECTIONS = 8
TOKENS = 2048
N_EXPERT = 32


def block_scale(key, extent, shards, low, top_value):
    level, own = 1.0, jax.random.fold_in(key, 6)
    for axis_at, parts in shards:
        heights = jnp.exp(jax.random.uniform(jax.random.fold_in(own, axis_at), (parts,), jnp.float32, low / len(shards), top_value / len(shards)))
        level = level * jnp.repeat(heights, extent[axis_at] // parts).reshape([-1 if axis == axis_at else 1 for axis in range(len(extent))])
    return level


def distinct(rng, rows, count, top, lift):
    sequence = jax.random.permutation(jax.random.fold_in(rng, 1), count)
    boost = sequence
    for power in range(3):
        boost = boost * boost // count
    boost = boost * lift // count
    tickets = jax.random.randint(jax.random.fold_in(rng, 2), (rows, count), 0, 4096) + boost
    sure = jax.random.permutation(jax.random.fold_in(rng, 3), rows)[jnp.arange(count) % rows]
    tickets = jnp.where(jnp.arange(rows)[:, None] == sure[None, :], 1 << 14, tickets)
    merit = tickets * count + jnp.arange(count)
    return lax.top_k(merit.astype(jnp.int32), top)[1].astype(jnp.int32)


def noise(rng, dims, deviation, limit, split=(), kind=jnp.bfloat16):
    values = deviation * jax.random.normal(rng, dims, jnp.float32)
    if split:
        values = values * block_scale(rng, dims, split, -0.22, 0.18)
    return jnp.clip(values, -limit, limit).astype(kind)


def setup_inputs(seed: int = 0) -> dict:
    keys = jax.random.split(jax.random.key(seed), 8)
    return {
        "acts": noise(keys[0], (SECTIONS, MICRO, TOKENS, D), 1.0, 6.0, ((0, 8), (2, 32))),
        "out_grad": noise(keys[1], (MICRO, TOKENS, D), 1.0, 6.0, ((1, 32),)),
        "w_gate": noise(keys[2], (SECTIONS, LIVE, D, H), D ** -0.5, 0.125, ((0, 8), (1, 32))),
        "w_up": noise(keys[3], (SECTIONS, LIVE, D, H), D ** -0.5, 0.125, ((0, 8), (1, 32))),
        "w_down": noise(keys[4], (SECTIONS, LIVE, H, D), H ** -0.5, 0.21875, ((0, 8), (1, 32))),
        "routes": distinct(keys[5], SECTIONS * MICRO * TOKENS, EXPERTS, TOP, 1024).reshape((SECTIONS, MICRO, TOKENS, TOP)),
        "gates": jnp.clip(0.2 + 0.400000021 * jax.random.uniform(keys[6], (SECTIONS, MICRO, TOKENS, TOP), jnp.float32) ** block_scale(keys[6], (SECTIONS, MICRO, TOKENS, TOP), ((0, 8), (2, 32)), -0.2, 0.2), 0.2, 0.6),
    }


def slot_tables(choose, weigh, live_count):
    choice_list = choose.reshape(-1)
    one_hot = (choice_list[:, None] == jnp.arange(EXPERTS, dtype=jnp.int32)[None, :]).astype(jnp.int32)
    before = jnp.cumsum(one_hot, axis=0).astype(jnp.int32) - one_hot
    slot_index = jnp.sum(before * one_hot, axis=1).astype(jnp.int32)
    kept_mask = (choice_list < live_count) & (slot_index < CAP)
    dump_slot = live_count * CAP
    slot_place = jnp.where(kept_mask, choice_list * CAP + slot_index, dump_slot).astype(jnp.int32)
    token_index = (jnp.arange(choice_list.shape[0], dtype=jnp.int32) // TOP).astype(jnp.int32)
    holder = jnp.full((dump_slot + 1,), choose.shape[0], jnp.int32).at[slot_place].set(token_index)
    kept_weight = jnp.where(kept_mask, weigh.reshape(-1), jnp.zeros_like(weigh.reshape(-1))).reshape(choose.shape)
    return holder[:dump_slot], slot_place.reshape(choose.shape), kept_weight


def dispatch_rows(token_block, slot_owner):
    padded = jnp.concatenate([token_block, jnp.zeros((1, token_block.shape[1]), token_block.dtype)], axis=0)
    return padded[slot_owner]


def expert_backward(operands):
    section_rows, grad_rows, gate_matrix, up_matrix, down_matrix = operands
    gate_pre = jnp.dot(section_rows, gate_matrix, preferred_element_type=jnp.float32)
    up_pre = jnp.dot(section_rows, up_matrix, preferred_element_type=jnp.float32)
    hidden_grad = lax.dot_general(grad_rows, down_matrix, (((1,), (1,)), ((), ())), preferred_element_type=jnp.float32)
    sigmoid_gate = jax.nn.sigmoid(gate_pre)
    gate_grad = (hidden_grad * up_pre * sigmoid_gate * (1.0 + gate_pre * (1.0 - sigmoid_gate))).astype(jnp.bfloat16)
    up_grad = (hidden_grad * gate_pre * sigmoid_gate).astype(jnp.bfloat16)
    summed = lax.dot_general(gate_grad, gate_matrix, (((1,), (1,)), ((), ())), preferred_element_type=jnp.float32)
    summed = summed + lax.dot_general(up_grad, up_matrix, (((1,), (1,)), ((), ())), preferred_element_type=jnp.float32)
    return summed.astype(jnp.bfloat16)


def combine_rows(returned, slot_place, kept_weight, incoming):
    padded = jnp.concatenate([returned, jnp.zeros((1, returned.shape[1]), returned.dtype)], axis=0)
    picked = padded[slot_place].astype(jnp.float32)
    summed = incoming.astype(jnp.float32) + jnp.einsum("tkd,tk->td", picked, kept_weight.astype(jnp.float32))
    return summed.astype(jnp.bfloat16)


def reference(acts, out_grad, w_gate, w_up, w_down, routes, gates):
    live_count = N_EXPERT
    tables = jax.vmap(partial(slot_tables, live_count=live_count))
    incoming_all = out_grad
    section_grads = []
    for section_index in range(SECTIONS - 1, -1, -1):
        micro_grads = []
        for micro_index in range(MICRO):
            slot_owner, slot_place, kept_weight = tables(
                routes[section_index, micro_index].reshape(N_EXPERT, TOK_DEV, TOP),
                gates[section_index, micro_index].reshape(N_EXPERT, TOK_DEV, TOP))
            section_block = acts[section_index, micro_index].reshape(N_EXPERT, TOK_DEV, D)
            grad_block = incoming_all[micro_index].reshape(N_EXPERT, TOK_DEV, D)
            sent_acts = jax.vmap(dispatch_rows)(section_block, slot_owner).reshape(N_EXPERT, live_count, CAP, D)
            sent_grads = jax.vmap(dispatch_rows)(grad_block, slot_owner).reshape(N_EXPERT, live_count, CAP, D)
            expert_acts = sent_acts.transpose(1, 0, 2, 3).reshape(live_count, N_EXPERT * CAP, D)
            expert_grads = sent_grads.transpose(1, 0, 2, 3).reshape(live_count, N_EXPERT * CAP, D)
            returned = lax.map(expert_backward, (expert_acts, expert_grads, w_gate[section_index], w_up[section_index], w_down[section_index]))
            returned = returned.reshape(live_count, N_EXPERT, CAP, D).transpose(1, 0, 2, 3).reshape(N_EXPERT, live_count * CAP, D)
            micro_grads.append(jax.vmap(combine_rows)(returned, slot_place, kept_weight, grad_block).reshape(TOKENS, D))
        incoming_all = jnp.stack(micro_grads)
        section_grads.append(incoming_all)
    return jnp.stack(section_grads[::-1])
```

```python
from functools import partial

import jax
import jax.numpy as jnp
from jax import lax
from jax.experimental import pallas as pl
from jax.experimental.pallas import tpu as pltpu
from jax.sharding import PartitionSpec as P

CAP = 6
PAD = 8
MESH = pl.DeviceIdType.MESH
F32 = jnp.float32
BF16 = jnp.bfloat16
NT = (((1,), (1,)), ((), ()))


def dot(a, b):
    return jnp.dot(a, b, preferred_element_type=F32)


def dot_nt(a, b):
    return lax.dot_general(a, b, NT, preferred_element_type=F32)


def kernel(
    sizes,
    acts,
    out_grad,
    w_gate,
    w_up,
    w_down,
    routes,
    gates,
    result,
    gate_w,
    up_w,
    down_w,
    own_acts,
    incoming,
    finished,
    own_pick,
    next_pick,
    blend,
    act_out,
    act_in,
    seed_out,
    grad_out,
    grad_in,
    row_out,
    row_in,
    stage,
    gate_coef,
    up_coef,
    hidden,
    weight_sem,
    load_sem,
    store_sem,
    pick_send,
    pick_recv,
    pass_send,
    pass_recv,
    act_send,
    act_recv,
    seed_send,
    grad_send,
    grad_recv,
    row_send,
    row_recv,
):
    sections, live, micro, tokens, width, chunks = sizes
    part = width // chunks
    slots = live * PAD
    section = lax.axis_index("pipe")
    mine = lax.axis_index("expert")
    first = section == sections - 1
    last = section == 0

    def local(src, dst, sem):
        return pltpu.make_async_copy(src, dst, sem)

    def arrived(ref, sem):
        pltpu.make_async_copy(ref, ref, sem).wait()

    def columns(c):
        return pl.ds(c * part, part)

    loads = [
        local(w_gate.at[0, 0], gate_w, weight_sem.at[0]),
        local(w_up.at[0, 0], up_w, weight_sem.at[1]),
        local(w_down.at[0, 0], down_w, weight_sem.at[2]),
    ]
    act_loads = [local(acts.at[0, m], own_acts.at[m], load_sem.at[m]) for m in range(micro)]
    for m in range(micro):
        act_loads[m].start()

    @pl.when(first)
    def _():
        for m in range(micro):
            local(out_grad.at[m], incoming.at[m], pass_recv.at[m]).start()

    for load in loads:
        load.start()

    stage[...] = jnp.zeros_like(stage)

    expert_of = lax.broadcasted_iota(jnp.int32, (tokens, live), 1)
    earlier = (
        lax.broadcasted_iota(jnp.int32, (tokens, tokens), 1)
        < lax.broadcasted_iota(jnp.int32, (tokens, tokens), 0)
    ).astype(F32).astype(BF16)
    spread = (
        lax.shift_right_logical(lax.broadcasted_iota(jnp.int32, (live, slots), 1), 3)
        == lax.broadcasted_iota(jnp.int32, (live, slots), 0)
    ).astype(F32)
    lane = lax.bitwise_and(lax.broadcasted_iota(jnp.int32, (tokens, slots), 1), PAD - 1)
    for m in range(micro):
        chosen = jnp.zeros((tokens, live), F32)
        weight = jnp.zeros((tokens, live), F32)
        for k in range(routes.shape[-1]):
            hit = routes[0, m, :, k : k + 1] == expert_of
            chosen = chosen + jnp.where(hit, 1.0, 0.0)
            weight = weight + jnp.where(hit, gates[0, m, :, k : k + 1], 0.0)
        slot = dot(earlier, chosen.astype(BF16))
        slot = dot(slot.astype(BF16), spread.astype(BF16))
        chosen = dot(chosen.astype(BF16), spread.astype(BF16))
        weight = jnp.dot(weight, spread, preferred_element_type=F32, precision=lax.Precision.HIGHEST)
        kept = (chosen > 0.5) & (jnp.abs(slot - lane.astype(F32)) < 0.5) & (lane < CAP)
        weight = jnp.where(kept, weight, 0.0)
        high = weight.astype(BF16)
        blend[m, 0:tokens, :] = high
        blend[m, tokens : 2 * tokens, :] = (weight - high.astype(F32)).astype(BF16)
        own_pick[m] = jnp.where(kept, 1.0, 0.0).T.astype(BF16)

    pick_copy = pltpu.make_async_remote_copy(
        own_pick,
        next_pick,
        pick_send,
        pick_recv,
        device_id=(jnp.minimum(section + 1, sections - 1), mine),
        device_id_type=MESH,
    )

    @pl.when(jnp.logical_not(first))
    def _():
        pick_copy.start()

    def send_slots(src, dst, m, c, target_section, send_sem, recv_sem, own):
        def one(i, carry):
            target = lax.rem(mine + i, live)
            pltpu.make_async_remote_copy(
                src.at[m, c, target],
                dst.at[m, c, mine],
                send_sem.at[m],
                recv_sem.at[m, c],
                device_id=(target_section, target),
                device_id_type=MESH,
            ).start()
            return carry

        if own:
            local(src.at[m, c, mine], dst.at[m, c, mine], recv_sem.at[m, c]).start()
        lax.fori_loop(1 if own else 0, live, one, 0)

    def sent(src, m, send_sem, own):
        for c in range(chunks):
            ref = src.at[m, c, pl.ds(0, live - 1)] if own else src.at[m, c]
            arrived(ref, send_sem.at[m])

    def put(dst, m, c, rows):
        dst[m, c] = rows.reshape(live, PAD, part)[:, :CAP, :].astype(BF16)

    def take(src, m, c):
        stage[c % 2, :, 0:CAP, :] = src[m, c].astype(F32)
        return stage[c % 2].reshape(slots, part).astype(BF16)

    for m in range(micro):
        act_loads[m].wait()
        for c in range(chunks):
            put(act_out, m, c, dot(own_pick[m], own_acts[m, :, columns(c)]))
            send_slots(act_out, act_in, m, c, section, act_send, act_recv, True)

        @pl.when(first)
        def _():
            arrived(incoming.at[m], pass_recv.at[m])
            for c in range(chunks):
                put(seed_out, m, c, dot(own_pick[m], incoming[m, :, columns(c)]))
                send_slots(seed_out, grad_in, m, c, section, seed_send, grad_recv, True)

    for load in loads:
        load.wait()

    def coefficients(m, carry):
        for c in range(chunks):
            arrived(act_in.at[m, c], act_recv.at[m, c])
            rows = take(act_in, m, c)
            gate_part = dot(rows, gate_w[columns(c), :])
            up_part = dot(rows, up_w[columns(c), :])
            if c == 0:
                gate_coef[m] = gate_part
                up_coef[m] = up_part
            else:
                gate_coef[m] += gate_part
                up_coef[m] += up_part
        gate_pre = gate_coef[m]
        up_pre = up_coef[m]
        sigmoid_gate = 1.0 / (1.0 + jnp.exp(-gate_pre))
        gate_coef[m] = up_pre * sigmoid_gate * (1.0 + gate_pre * (1.0 - sigmoid_gate))
        up_coef[m] = gate_pre * sigmoid_gate
        return carry

    lax.fori_loop(0, micro, coefficients, 0)

    @pl.when(jnp.logical_not(last))
    def _():
        arrived(next_pick, pick_recv)

    def step(m, carry):
        for c in range(chunks):
            arrived(grad_in.at[m, c], grad_recv.at[m, c])
            hidden_part = dot_nt(take(grad_in, m, c), down_w[:, columns(c)])
            if c == 0:
                hidden[...] = hidden_part
            else:
                hidden[...] += hidden_part
        hidden_grad = hidden[...]
        gate_grad = (hidden_grad * gate_coef[m]).astype(BF16)
        up_grad = (hidden_grad * up_coef[m]).astype(BF16)
        for c in range(chunks):
            rows = dot_nt(gate_grad, gate_w[columns(c), :]) + dot_nt(up_grad, up_w[columns(c), :])
            put(row_out, m, c, rows)
            send_slots(row_out, row_in, m, c, section, row_send, row_recv, True)

        @pl.when(jnp.logical_not(first))
        def _():
            arrived(incoming.at[m], pass_recv.at[m])

        for c in range(chunks):
            arrived(row_in.at[m, c], row_recv.at[m, c])
            both = dot(blend[m], take(row_in, m, c))
            total = incoming[m, :, columns(c)].astype(F32) + (both[:tokens] + both[tokens:])
            total = total.astype(BF16)
            finished[m, :, columns(c)] = total

            @pl.when(jnp.logical_not(last))
            def _():
                put(grad_out, m, c, dot(next_pick[m], total))
                send_slots(grad_out, grad_in, m, c, section - 1, grad_send, grad_recv, False)

        @pl.when(jnp.logical_not(last))
        def _():
            pltpu.make_async_remote_copy(
                finished.at[m],
                incoming.at[m],
                pass_send.at[m],
                pass_recv.at[m],
                device_id=(section - 1, mine),
                device_id_type=MESH,
            ).start()

        local(finished.at[m], result.at[0, m], store_sem.at[m]).start()
        return carry

    lax.fori_loop(0, micro, step, 0)

    @pl.when(jnp.logical_not(first))
    def _():
        pick_copy.wait_send()

    for m in range(micro):
        sent(act_out, m, act_send, True)
        sent(row_out, m, row_send, True)
        arrived(finished.at[m], store_sem.at[m])

        @pl.when(first)
        def _():
            sent(seed_out, m, seed_send, True)

        @pl.when(jnp.logical_not(last))
        def _():
            arrived(finished.at[m], pass_send.at[m])
            sent(grad_out, m, grad_send, False)


def shards(chunks, acts, out_grad, w_gate, w_up, w_down, routes, gates):
    sections = lax.axis_size("pipe")
    live = lax.axis_size("expert")
    micro, tokens, width = acts.shape[1:]
    units = w_gate.shape[-1]
    part = width // chunks
    slots = live * PAD
    sizes = (sections, live, micro, tokens, width, chunks)
    slab = pltpu.VMEM((micro, chunks, live, CAP, part), BF16)
    block = pltpu.VMEM((micro, tokens, width), BF16)
    sems = pltpu.SemaphoreType.DMA((micro,))
    chunk_sems = pltpu.SemaphoreType.DMA((micro, chunks))
    whole = pl.BlockSpec(memory_space=pltpu.VMEM)
    place = pl.BlockSpec(memory_space=pl.ANY)
    return pl.pallas_call(
        partial(kernel, sizes),
        out_shape=jax.ShapeDtypeStruct(acts.shape, BF16),
        in_specs=[place] * 5 + [whole] * 2,
        out_specs=place,
        scratch_shapes=[
            pltpu.VMEM((width, units), BF16),
            pltpu.VMEM((width, units), BF16),
            pltpu.VMEM((units, width), BF16),
            block,
            block,
            block,
            pltpu.VMEM((micro, slots, tokens), BF16),
            pltpu.VMEM((micro, slots, tokens), BF16),
            pltpu.VMEM((micro, 2 * tokens, slots), BF16),
            slab,
            slab,
            slab,
            slab,
            slab,
            slab,
            slab,
            pltpu.VMEM((2, live, PAD, part), F32),
            pltpu.VMEM((micro, slots, units), F32),
            pltpu.VMEM((micro, slots, units), F32),
            pltpu.VMEM((slots, units), F32),
            pltpu.SemaphoreType.DMA((3,)),
            sems,
            sems,
            pltpu.SemaphoreType.DMA,
            pltpu.SemaphoreType.DMA,
            sems,
            sems,
            sems,
            chunk_sems,
            sems,
            sems,
            chunk_sems,
            sems,
            chunk_sems,
        ],
        compiler_params=pltpu.CompilerParams(
            has_side_effects=True, vmem_limit_bytes=60 * 1024 * 1024
        ),
    )(acts, out_grad, w_gate, w_up, w_down, routes, gates)


def solution(mesh, chunks=4):
    return jax.shard_map(
        partial(shards, chunks),
        mesh=mesh,
        in_specs=(
            P("pipe", None, "expert", None),
            P(None, "expert", None),
            P("pipe", "expert", None, None),
            P("pipe", "expert", None, None),
            P("pipe", "expert", None, None),
            P("pipe", None, "expert", None),
            P("pipe", None, "expert", None),
        ),
        out_specs=P("pipe", None, "expert", None),
        check_vma=False,
    )
```

```python
from functools import partial

import jax
import jax.numpy as jnp
from jax import lax
from jax.experimental import pallas as pl
from jax.experimental.pallas import tpu as pltpu
from jax.sharding import PartitionSpec as P

CAP = 6
PAD = 8
LANES = 128
MESH = pl.DeviceIdType.MESH
F32 = jnp.float32
BF16 = jnp.bfloat16
NT = (((1,), (1,)), ((), ()))


def dot(a, b):
    return jnp.dot(a, b, preferred_element_type=F32)


def dot_nt(a, b):
    return lax.dot_general(a, b, NT, preferred_element_type=F32)


def kernel(
    sizes,
    acts,
    out_grad,
    w_gate,
    w_up,
    w_down,
    routes,
    gates,
    result,
    gate_w,
    up_w,
    down_w,
    own_acts,
    incoming,
    finished,
    own_pick,
    next_pick,
    blend,
    act_out,
    act_in,
    seed_out,
    grad_out,
    grad_in,
    row_out,
    row_in,
    gate_coef,
    up_coef,
    hidden,
    weight_sem,
    load_sem,
    store_sem,
    pick_send,
    pick_recv,
    pass_send,
    pass_recv,
    act_send,
    act_recv,
    seed_send,
    grad_send,
    grad_recv,
    row_send,
    row_recv,
):
    sections, live, micro, tokens, width, chunks = sizes
    part = width // chunks
    slots = live * PAD
    section = lax.axis_index("pipe")
    mine = lax.axis_index("expert")
    first = section == sections - 1
    last = section == 0

    def local(src, dst, sem):
        return pltpu.make_async_copy(src, dst, sem)

    def arrived(ref, sem):
        pltpu.make_async_copy(ref, ref, sem).wait()

    def columns(c):
        return pl.ds(c * part, part)

    loads = [
        local(w_gate.at[0, 0], gate_w, weight_sem.at[0]),
        local(w_up.at[0, 0], up_w, weight_sem.at[1]),
        local(w_down.at[0, 0], down_w, weight_sem.at[2]),
    ]
    act_loads = [local(acts.at[0, m], own_acts.at[m], load_sem.at[m]) for m in range(micro)]
    for m in range(micro):
        act_loads[m].start()

    @pl.when(first)
    def _():
        for m in range(micro):
            local(out_grad.at[m], incoming.at[m], pass_recv.at[m]).start()

    for load in loads:
        load.start()

    slot_row = lax.broadcasted_iota(jnp.int32, (live, PAD, LANES), 1)
    low_rows = slot_row < CAP

    expert_of = lax.broadcasted_iota(jnp.int32, (tokens, live), 1)
    earlier = (
        lax.broadcasted_iota(jnp.int32, (tokens, tokens), 1)
        < lax.broadcasted_iota(jnp.int32, (tokens, tokens), 0)
    ).astype(F32).astype(BF16)
    spread = (
        lax.shift_right_logical(lax.broadcasted_iota(jnp.int32, (live, slots), 1), 3)
        == lax.broadcasted_iota(jnp.int32, (live, slots), 0)
    ).astype(F32)
    lane = lax.bitwise_and(lax.broadcasted_iota(jnp.int32, (tokens, slots), 1), PAD - 1)
    for m in range(micro):
        chosen = jnp.zeros((tokens, live), F32)
        weight = jnp.zeros((tokens, live), F32)
        for k in range(routes.shape[-1]):
            hit = routes[0, m, :, k : k + 1] == expert_of
            chosen = chosen + jnp.where(hit, 1.0, 0.0)
            weight = weight + jnp.where(hit, gates[0, m, :, k : k + 1], 0.0)
        slot = dot(earlier, chosen.astype(BF16))
        slot = dot(slot.astype(BF16), spread.astype(BF16))
        chosen = dot(chosen.astype(BF16), spread.astype(BF16))
        weight = jnp.dot(weight, spread, preferred_element_type=F32, precision=lax.Precision.HIGHEST)
        kept = (chosen > 0.5) & (jnp.abs(slot - lane.astype(F32)) < 0.5) & (lane < CAP)
        weight = jnp.where(kept, weight, 0.0)
        high = weight.astype(BF16)
        blend[m, 0:tokens, :] = high
        blend[m, tokens : 2 * tokens, :] = (weight - high.astype(F32)).astype(BF16)
        own_pick[m] = jnp.where(kept, 1.0, 0.0).T.astype(BF16)

    pick_copy = pltpu.make_async_remote_copy(
        own_pick,
        next_pick,
        pick_send,
        pick_recv,
        device_id=(jnp.minimum(section + 1, sections - 1), mine),
        device_id_type=MESH,
    )

    @pl.when(jnp.logical_not(first))
    def _():
        pick_copy.start()

    def send_slots(src, dst, m, c, target_section, send_sem, recv_sem, own):
        def one(i, carry):
            target = lax.rem(mine + i, live)
            pltpu.make_async_remote_copy(
                src.at[m, c, target],
                dst.at[m, c, mine],
                send_sem.at[m],
                recv_sem.at[m, c],
                device_id=(target_section, target),
                device_id_type=MESH,
            ).start()
            return carry

        if own:
            local(src.at[m, c, mine], dst.at[m, c, mine], recv_sem.at[m, c]).start()
        lax.fori_loop(1 if own else 0, live, one, 0)

    def sent(src, m, send_sem, own):
        for c in range(chunks):
            ref = src.at[m, c, pl.ds(0, live - 1)] if own else src.at[m, c]
            arrived(ref, send_sem.at[m])

    def put(dst, m, c, rows):
        rows = rows.reshape(live, PAD, part)
        rest = rows[:, :, CAP // 2 * LANES :]
        for j in range(CAP // 2):
            moved = pltpu.roll(rest, CAP - 2 * j, 1)
            tile = jnp.where(low_rows, rows[:, :, j * LANES : (j + 1) * LANES], moved)
            dst[m, c, :, :, j * LANES : (j + 1) * LANES] = tile.astype(BF16)

    def take(src, m, c):
        packed = src[m, c].astype(F32)
        rest = jnp.zeros((live, PAD, LANES), F32)
        for j in range(CAP // 2):
            moved = pltpu.roll(packed[:, :, j * LANES : (j + 1) * LANES], PAD - CAP + 2 * j, 1)
            rest = jnp.where(slot_row // 2 == j, moved, rest)
        rows = jnp.concatenate([packed, rest], axis=2)
        return rows.reshape(slots, part).astype(BF16)

    for m in range(micro):
        act_loads[m].wait()
        for c in range(chunks):
            put(act_out, m, c, dot(own_pick[m], own_acts[m, :, columns(c)]))
            send_slots(act_out, act_in, m, c, section, act_send, act_recv, True)

        @pl.when(first)
        def _():
            arrived(incoming.at[m], pass_recv.at[m])
            for c in range(chunks):
                put(seed_out, m, c, dot(own_pick[m], incoming[m, :, columns(c)]))
                send_slots(seed_out, grad_in, m, c, section, seed_send, grad_recv, True)

    for load in loads:
        load.wait()

    def coefficients(m, carry):
        for c in range(chunks):
            arrived(act_in.at[m, c], act_recv.at[m, c])
            rows = take(act_in, m, c)
            gate_part = dot(rows, gate_w[columns(c), :])
            up_part = dot(rows, up_w[columns(c), :])
            if c == 0:
                gate_coef[m] = gate_part
                up_coef[m] = up_part
            else:
                gate_coef[m] += gate_part
                up_coef[m] += up_part
        gate_pre = gate_coef[m]
        up_pre = up_coef[m]
        sigmoid_gate = 1.0 / (1.0 + jnp.exp(-gate_pre))
        gate_coef[m] = up_pre * sigmoid_gate * (1.0 + gate_pre * (1.0 - sigmoid_gate))
        up_coef[m] = gate_pre * sigmoid_gate
        return carry

    lax.fori_loop(0, micro, coefficients, 0)

    @pl.when(jnp.logical_not(last))
    def _():
        arrived(next_pick, pick_recv)

    def step(m, carry):
        for c in range(chunks):
            arrived(grad_in.at[m, c], grad_recv.at[m, c])
            hidden_part = dot_nt(take(grad_in, m, c), down_w[:, columns(c)])
            if c == 0:
                hidden[...] = hidden_part
            else:
                hidden[...] += hidden_part
        hidden_grad = hidden[...]
        gate_grad = (hidden_grad * gate_coef[m]).astype(BF16)
        up_grad = (hidden_grad * up_coef[m]).astype(BF16)
        for c in range(chunks):
            rows = dot_nt(gate_grad, gate_w[columns(c), :]) + dot_nt(up_grad, up_w[columns(c), :])
            put(row_out, m, c, rows)
            send_slots(row_out, row_in, m, c, section, row_send, row_recv, True)

        @pl.when(jnp.logical_not(first))
        def _():
            arrived(incoming.at[m], pass_recv.at[m])

        for c in range(chunks):
            arrived(row_in.at[m, c], row_recv.at[m, c])
            both = dot(blend[m], take(row_in, m, c))
            total = incoming[m, :, columns(c)].astype(F32) + (both[:tokens] + both[tokens:])
            total = total.astype(BF16)
            finished[m, :, columns(c)] = total

            @pl.when(jnp.logical_not(last))
            def _():
                put(grad_out, m, c, dot(next_pick[m], total))
                send_slots(grad_out, grad_in, m, c, section - 1, grad_send, grad_recv, False)

        @pl.when(jnp.logical_not(last))
        def _():
            pltpu.make_async_remote_copy(
                finished.at[m],
                incoming.at[m],
                pass_send.at[m],
                pass_recv.at[m],
                device_id=(section - 1, mine),
                device_id_type=MESH,
            ).start()

        local(finished.at[m], result.at[0, m], store_sem.at[m]).start()
        return carry

    lax.fori_loop(0, micro, step, 0)

    @pl.when(jnp.logical_not(first))
    def _():
        pick_copy.wait_send()

    for m in range(micro):
        sent(act_out, m, act_send, True)
        sent(row_out, m, row_send, True)
        arrived(finished.at[m], store_sem.at[m])

        @pl.when(first)
        def _():
            sent(seed_out, m, seed_send, True)

        @pl.when(jnp.logical_not(last))
        def _():
            arrived(finished.at[m], pass_send.at[m])
            sent(grad_out, m, grad_send, False)


def shards(chunks, acts, out_grad, w_gate, w_up, w_down, routes, gates):
    sections = lax.axis_size("pipe")
    live = lax.axis_size("expert")
    micro, tokens, width = acts.shape[1:]
    units = w_gate.shape[-1]
    part = width // chunks
    slots = live * PAD
    sizes = (sections, live, micro, tokens, width, chunks)
    slab = pltpu.VMEM((micro, chunks, live, PAD, part * CAP // PAD), BF16)
    block = pltpu.VMEM((micro, tokens, width), BF16)
    sems = pltpu.SemaphoreType.DMA((micro,))
    chunk_sems = pltpu.SemaphoreType.DMA((micro, chunks))
    whole = pl.BlockSpec(memory_space=pltpu.VMEM)
    place = pl.BlockSpec(memory_space=pl.ANY)
    return pl.pallas_call(
        partial(kernel, sizes),
        out_shape=jax.ShapeDtypeStruct(acts.shape, BF16),
        in_specs=[place] * 5 + [whole] * 2,
        out_specs=place,
        scratch_shapes=[
            pltpu.VMEM((width, units), BF16),
            pltpu.VMEM((width, units), BF16),
            pltpu.VMEM((units, width), BF16),
            block,
            block,
            block,
            pltpu.VMEM((micro, slots, tokens), BF16),
            pltpu.VMEM((micro, slots, tokens), BF16),
            pltpu.VMEM((micro, 2 * tokens, slots), BF16),
            slab,
            slab,
            slab,
            slab,
            slab,
            slab,
            slab,
            pltpu.VMEM((micro, slots, units), F32),
            pltpu.VMEM((micro, slots, units), F32),
            pltpu.VMEM((slots, units), F32),
            pltpu.SemaphoreType.DMA((3,)),
            sems,
            sems,
            pltpu.SemaphoreType.DMA,
            pltpu.SemaphoreType.DMA,
            sems,
            sems,
            sems,
            chunk_sems,
            sems,
            sems,
            chunk_sems,
            sems,
            chunk_sems,
        ],
        compiler_params=pltpu.CompilerParams(
            has_side_effects=True, vmem_limit_bytes=60 * 1024 * 1024
        ),
    )(acts, out_grad, w_gate, w_up, w_down, routes, gates)


def solution(mesh, chunks=4):
    return jax.shard_map(
        partial(shards, chunks),
        mesh=mesh,
        in_specs=(
            P("pipe", None, "expert", None),
            P(None, "expert", None),
            P("pipe", "expert", None, None),
            P("pipe", "expert", None, None),
            P("pipe", "expert", None, None),
            P("pipe", None, "expert", None),
            P("pipe", None, "expert", None),
        ),
        out_specs=P("pipe", None, "expert", None),
        check_vma=False,
    )
```

```python
from functools import partial

import jax
import jax.numpy as jnp
from jax import lax
from jax.experimental import pallas as pl
from jax.experimental.pallas import tpu as pltpu
from jax.sharding import PartitionSpec as P

CAP = 6
PAD = 8
LANES = 128
MESH = pl.DeviceIdType.MESH
F32 = jnp.float32
BF16 = jnp.bfloat16
NT = (((1,), (1,)), ((), ()))


def dot(a, b):
    return jnp.dot(a, b, preferred_element_type=F32)


def dot_nt(a, b):
    return lax.dot_general(a, b, NT, preferred_element_type=F32)


def kernel(
    sizes,
    acts,
    out_grad,
    w_gate,
    w_up,
    w_down,
    routes,
    gates,
    result,
    gate_w,
    up_w,
    down_w,
    own_acts,
    incoming,
    finished,
    own_pick,
    next_pick,
    blend,
    act_out,
    act_in,
    seed_out,
    grad_out,
    grad_in,
    row_out,
    row_in,
    gate_coef,
    up_coef,
    hidden,
    weight_sem,
    load_sem,
    store_sem,
    pick_send,
    pick_recv,
    pass_send,
    pass_recv,
    act_send,
    act_recv,
    seed_send,
    grad_send,
    grad_recv,
    row_send,
    row_recv,
    turn,
):
    sections, live, micro, tokens, width, chunks = sizes
    part = width // chunks
    slots = live * PAD
    section = lax.axis_index("pipe")
    mine = lax.axis_index("expert")
    first = section == sections - 1
    last = section == 0

    def local(src, dst, sem):
        return pltpu.make_async_copy(src, dst, sem)

    def arrived(ref, sem):
        pltpu.make_async_copy(ref, ref, sem).wait()

    def columns(c):
        return pl.ds(c * part, part)

    loads = [
        local(w_gate.at[0, 0], gate_w, weight_sem.at[0]),
        local(w_up.at[0, 0], up_w, weight_sem.at[1]),
        local(w_down.at[0, 0], down_w, weight_sem.at[2]),
    ]
    act_loads = [local(acts.at[0, m], own_acts.at[m], load_sem.at[m]) for m in range(micro)]
    for m in range(micro):
        act_loads[m].start()

    @pl.when(first)
    def _():
        for m in range(micro):
            local(out_grad.at[m], incoming.at[m], pass_recv.at[m]).start()

    for load in loads:
        load.start()

    slot_row = lax.broadcasted_iota(jnp.int32, (live, PAD, LANES), 1)
    low_rows = slot_row < CAP

    expert_of = lax.broadcasted_iota(jnp.int32, (tokens, live), 1)
    earlier = (
        lax.broadcasted_iota(jnp.int32, (tokens, tokens), 1)
        < lax.broadcasted_iota(jnp.int32, (tokens, tokens), 0)
    ).astype(F32).astype(BF16)
    spread = (
        lax.shift_right_logical(lax.broadcasted_iota(jnp.int32, (live, slots), 1), 3)
        == lax.broadcasted_iota(jnp.int32, (live, slots), 0)
    ).astype(F32)
    lane = lax.bitwise_and(lax.broadcasted_iota(jnp.int32, (tokens, slots), 1), PAD - 1)
    for m in range(micro):
        chosen = jnp.zeros((tokens, live), F32)
        weight = jnp.zeros((tokens, live), F32)
        for k in range(routes.shape[-1]):
            hit = routes[0, m, :, k : k + 1] == expert_of
            chosen = chosen + jnp.where(hit, 1.0, 0.0)
            weight = weight + jnp.where(hit, gates[0, m, :, k : k + 1], 0.0)
        slot = dot(earlier, chosen.astype(BF16))
        slot = dot(slot.astype(BF16), spread.astype(BF16))
        chosen = dot(chosen.astype(BF16), spread.astype(BF16))
        weight = jnp.dot(weight, spread, preferred_element_type=F32, precision=lax.Precision.HIGHEST)
        kept = (chosen > 0.5) & (jnp.abs(slot - lane.astype(F32)) < 0.5) & (lane < CAP)
        weight = jnp.where(kept, weight, 0.0)
        high = weight.astype(BF16)
        blend[m, 0:tokens, :] = high
        blend[m, tokens : 2 * tokens, :] = (weight - high.astype(F32)).astype(BF16)
        own_pick[m] = jnp.where(kept, 1.0, 0.0).T.astype(BF16)

    pick_copy = pltpu.make_async_remote_copy(
        own_pick,
        next_pick,
        pick_send,
        pick_recv,
        device_id=(jnp.minimum(section + 1, sections - 1), mine),
        device_id_type=MESH,
    )

    @pl.when(jnp.logical_not(first))
    def _():
        pick_copy.start()

    def send_slots(src, dst, m, c, target_section, send_sem, recv_sem, own):
        def one(i, carry):
            target = lax.rem(mine + i, live)
            pltpu.make_async_remote_copy(
                src.at[m, c, target],
                dst.at[m, c, mine],
                send_sem.at[m],
                recv_sem.at[m, c],
                device_id=(target_section, target),
                device_id_type=MESH,
            ).start()
            return carry

        if own:
            local(src.at[m, c, mine], dst.at[m, c, mine], recv_sem.at[m, c]).start()
        lax.fori_loop(1 if own else 0, live, one, 0)

    def sent(src, m, send_sem, own):
        for c in range(chunks):
            ref = src.at[m, c, pl.ds(0, live - 1)] if own else src.at[m, c]
            arrived(ref, send_sem.at[m])

    def put(dst, m, c, rows):
        rows = rows.reshape(live, PAD, part)
        rest = rows[:, :, CAP // 2 * LANES :]
        for j in range(CAP // 2):
            moved = pltpu.roll(rest, CAP - 2 * j, 1)
            tile = jnp.where(low_rows, rows[:, :, j * LANES : (j + 1) * LANES], moved)
            dst[m, c, :, :, j * LANES : (j + 1) * LANES] = tile.astype(BF16)

    def take(src, m, c):
        packed = src[m, c].astype(F32)
        rest = jnp.zeros((live, PAD, LANES), F32)
        for j in range(CAP // 2):
            moved = pltpu.roll(packed[:, :, j * LANES : (j + 1) * LANES], PAD - CAP + 2 * j, 1)
            rest = jnp.where(slot_row // 2 == j, moved, rest)
        rows = jnp.concatenate([packed, rest], axis=2)
        return rows.reshape(slots, part).astype(BF16)

    for m in range(micro):
        act_loads[m].wait()
        for c in range(chunks):
            put(act_out, m, c, dot(own_pick[m], own_acts[m, :, columns(c)]))
            send_slots(act_out, act_in, m, c, section, act_send, act_recv, True)

        @pl.when(first)
        def _():
            arrived(incoming.at[m], pass_recv.at[m])
            for c in range(chunks):
                put(seed_out, m, c, dot(own_pick[m], incoming[m, :, columns(c)]))
                send_slots(seed_out, grad_in, m, c, section, seed_send, grad_recv, True)

    for load in loads:
        load.wait()

    def coefficients(m, carry):
        for c in range(chunks):
            arrived(act_in.at[m, c], act_recv.at[m, c])
            rows = take(act_in, m, c)
            gate_part = dot(rows, gate_w[columns(c), :])
            up_part = dot(rows, up_w[columns(c), :])
            if c == 0:
                gate_coef[m] = gate_part
                up_coef[m] = up_part
            else:
                gate_coef[m] += gate_part
                up_coef[m] += up_part
        gate_pre = gate_coef[m]
        up_pre = up_coef[m]
        sigmoid_gate = 1.0 / (1.0 + jnp.exp(-gate_pre))
        gate_coef[m] = up_pre * sigmoid_gate * (1.0 + gate_pre * (1.0 - sigmoid_gate))
        up_coef[m] = gate_pre * sigmoid_gate
        return carry

    lax.fori_loop(0, micro, coefficients, 0)

    @pl.when(jnp.logical_not(last))
    def _():
        arrived(next_pick, pick_recv)

    def step(m, carry):
        for c in range(chunks):
            arrived(grad_in.at[m, c], grad_recv.at[m, c])
            hidden_part = dot_nt(take(grad_in, m, c), down_w[:, columns(c)])
            if c == 0:
                hidden[...] = hidden_part
            else:
                hidden[...] += hidden_part
        hidden_grad = hidden[...]

        @pl.when((m == 1) & (lax.rem(section, 2) == 1))
        def _():
            pl.semaphore_wait(turn, 1)

        gate_grad = (hidden_grad * gate_coef[m]).astype(BF16)
        up_grad = (hidden_grad * up_coef[m]).astype(BF16)
        for c in range(chunks):
            rows = dot_nt(gate_grad, gate_w[columns(c), :]) + dot_nt(up_grad, up_w[columns(c), :])
            put(row_out, m, c, rows)
            send_slots(row_out, row_in, m, c, section, row_send, row_recv, True)

        @pl.when(jnp.logical_not(first))
        def _():
            arrived(incoming.at[m], pass_recv.at[m])

        for c in range(chunks):
            arrived(row_in.at[m, c], row_recv.at[m, c])
            both = dot(blend[m], take(row_in, m, c))
            total = incoming[m, :, columns(c)].astype(F32) + (both[:tokens] + both[tokens:])
            total = total.astype(BF16)
            finished[m, :, columns(c)] = total

            @pl.when(jnp.logical_not(last))
            def _():
                put(grad_out, m, c, dot(next_pick[m], total))
                send_slots(grad_out, grad_in, m, c, section - 1, grad_send, grad_recv, False)

        @pl.when(jnp.logical_not(last))
        def _():
            pltpu.make_async_remote_copy(
                finished.at[m],
                incoming.at[m],
                pass_send.at[m],
                pass_recv.at[m],
                device_id=(section - 1, mine),
                device_id_type=MESH,
            ).start()

        local(finished.at[m], result.at[0, m], store_sem.at[m]).start()

        @pl.when((m == 0) & (lax.rem(section, 2) == 0))
        def _():
            pl.semaphore_signal(turn, inc=1, device_id=(section + 1, mine), device_id_type=MESH)

        return carry

    lax.fori_loop(0, micro, step, 0)

    @pl.when(jnp.logical_not(first))
    def _():
        pick_copy.wait_send()

    for m in range(micro):
        sent(act_out, m, act_send, True)
        sent(row_out, m, row_send, True)
        arrived(finished.at[m], store_sem.at[m])

        @pl.when(first)
        def _():
            sent(seed_out, m, seed_send, True)

        @pl.when(jnp.logical_not(last))
        def _():
            arrived(finished.at[m], pass_send.at[m])
            sent(grad_out, m, grad_send, False)


def shards(chunks, acts, out_grad, w_gate, w_up, w_down, routes, gates):
    sections = lax.axis_size("pipe")
    live = lax.axis_size("expert")
    micro, tokens, width = acts.shape[1:]
    units = w_gate.shape[-1]
    part = width // chunks
    slots = live * PAD
    sizes = (sections, live, micro, tokens, width, chunks)
    slab = pltpu.VMEM((micro, chunks, live, PAD, part * CAP // PAD), BF16)
    block = pltpu.VMEM((micro, tokens, width), BF16)
    sems = pltpu.SemaphoreType.DMA((micro,))
    chunk_sems = pltpu.SemaphoreType.DMA((micro, chunks))
    whole = pl.BlockSpec(memory_space=pltpu.VMEM)
    place = pl.BlockSpec(memory_space=pl.ANY)
    return pl.pallas_call(
        partial(kernel, sizes),
        out_shape=jax.ShapeDtypeStruct(acts.shape, BF16),
        in_specs=[place] * 5 + [whole] * 2,
        out_specs=place,
        scratch_shapes=[
            pltpu.VMEM((width, units), BF16),
            pltpu.VMEM((width, units), BF16),
            pltpu.VMEM((units, width), BF16),
            block,
            block,
            block,
            pltpu.VMEM((micro, slots, tokens), BF16),
            pltpu.VMEM((micro, slots, tokens), BF16),
            pltpu.VMEM((micro, 2 * tokens, slots), BF16),
            slab,
            slab,
            slab,
            slab,
            slab,
            slab,
            slab,
            pltpu.VMEM((micro, slots, units), F32),
            pltpu.VMEM((micro, slots, units), F32),
            pltpu.VMEM((slots, units), F32),
            pltpu.SemaphoreType.DMA((3,)),
            sems,
            sems,
            pltpu.SemaphoreType.DMA,
            pltpu.SemaphoreType.DMA,
            sems,
            sems,
            sems,
            chunk_sems,
            sems,
            sems,
            chunk_sems,
            sems,
            chunk_sems,
            pltpu.SemaphoreType.REGULAR,
        ],
        compiler_params=pltpu.CompilerParams(
            has_side_effects=True, vmem_limit_bytes=60 * 1024 * 1024
        ),
    )(acts, out_grad, w_gate, w_up, w_down, routes, gates)


def solution(mesh, chunks=4):
    return jax.shard_map(
        partial(shards, chunks),
        mesh=mesh,
        in_specs=(
            P("pipe", None, "expert", None),
            P(None, "expert", None),
            P("pipe", "expert", None, None),
            P("pipe", "expert", None, None),
            P("pipe", "expert", None, None),
            P("pipe", None, "expert", None),
            P("pipe", None, "expert", None),
        ),
        out_specs=P("pipe", None, "expert", None),
        check_vma=False,
    )
```
